256 devices in a mesh: grp: 8 (over z), tok: 32 (over y, x, core).
Axes of the slice: x: 4, y: 4, z: 8, core: 2. Of those that a mesh axis runs over, the one named last changes fastest.
Arguments:
- residual_in: bfloat16 [8192, 2048], P(('tok', 'grp')), may hold values from -2.5 to 2.5
- queries: bfloat16 [8192, 2048], P('tok', 'grp'), may hold values from -120 to 120
- fresh_pairs: bfloat16 [8192, 2048], P('tok'), may hold values from -6 to 6
- cache_pairs: bfloat16 [16384, 2048], P('tok'), may hold values from -6 to 6
- segment_ids: int32 [8192], replicated, may hold values from 0 to 15, never falling along the last dimension, each value on 1 to 4096 neighbouring positions
- prefix_length: int32 [16], replicated, may hold values from 0 to 256, as said below
- page_order: int32 [1024], replicated, may hold values from 0 to 1023, each once
- out_weight: bfloat16 [2048, 2048], P('grp'), may hold values from -0.125 to 0.125
- post_gain: float32 [2048], replicated, may hold values from 0.25 to 1.75
- gate_weight: bfloat16 [2048, 4096], P(None, 'grp'), may hold values from -0.125 to 0.125
- up_weight: bfloat16 [2048, 4096], P(None, 'grp'), may hold values from -0.125 to 0.125
- down_weight: bfloat16 [4096, 2048], P('grp'), may hold values from -0.09375 to 0.09375
- next_gain: float32 [2048], replicated, may hold values from 0.25 to 1.75
- next_weight: bfloat16 [2048, 4096], P(None, 'grp'), may hold values from -0.125 to 0.125
Outputs:
- attended: bfloat16 [8192, 2048], P('tok', 'grp')
- new_cache: bfloat16 [16384, 2048], P('tok', 'grp')
- layer_out: bfloat16 [8192, 2048], P(('tok', 'grp'))
- next_proj: bfloat16 [8192, 4096], P('tok', 'grp')
The draws below stay inside these ranges and needn't reach their ends.
Inputs may be any that keep to these rules, and one draw needn't show every extreme that they name: `segment_ids`: segment numbers never fall along the stream; each of the 16 segments has 1 to 4096 tokens and one has exactly 4096. `prefix_length`: one segment has exactly 256 cached tokens. `page_order`: each page number appears once.
All inputs are finite; a program needn't handle non-finite values.
Results may differ from the reference program's by a relative error of at most 0.024.
Values may be sent and summed in bfloat16 or wider, within the bound.
A program may use at most 128 MiB of HBM per device.

```python
import math
import jax
import jax.numpy as jnp
import numpy as np
from jax import lax

D = 2048
HEADS = 8
KV_HEADS = 4
HD = 256
FF = 4096
PAGE = 16
STREAM = 8192
SEGS = 16
SEG_MAX = 4096
PREFIX_MAX = 256
CACHE = 16384
NPAGES = 1024


def shared_rows(key):
    first = jax.random.fold_in(key, 11)
    keys_raw = jnp.clip(jax.random.normal(jax.random.fold_in(first, 1), (STREAM, KV_HEADS, HD), jnp.float32), -6.0, 6.0)
    values_raw = jnp.clip(jax.random.normal(jax.random.fold_in(first, 2), (STREAM, KV_HEADS, HD), jnp.float32), -6.0, 6.0)
    query_raw = jnp.clip(jax.random.normal(jax.random.fold_in(first, 3), (STREAM, KV_HEADS, HEADS // KV_HEADS, HD), jnp.float32), -6.0, 6.0)
    return (query_raw, keys_raw, values_raw)


def draw_queries(key, part):
    query_raw, keys_raw, values_raw = shared_rows(key)
    return query_raw.reshape(STREAM, HEADS * HD).astype(jnp.bfloat16)


def draw_fresh_pairs(key, part):
    query_raw, keys_raw, values_raw = shared_rows(key)
    stacked = jnp.stack([keys_raw, values_raw], axis=2)
    return stacked.reshape(STREAM, 2 * KV_HEADS * HD).astype(jnp.bfloat16)


def draw_prefix_length(key, part):
    lengths = jax.random.randint(jax.random.fold_in(key, 21), (SEGS,), 0, PREFIX_MAX + 1)
    keeping = jax.random.randint(jax.random.fold_in(key, 22), (SEGS,), 0, 3) > 0
    picked = jax.random.randint(jax.random.fold_in(key, 23), (), 0, SEGS)
    lengths = jnp.where(keeping, lengths, 0)
    return jnp.where(jnp.arange(SEGS) == picked, PREFIX_MAX, lengths).astype(jnp.int32)


def block_scale(stream_key, extent, cuts, least, largest):
    level = 1.0
    for dim, parts in cuts:
        draws = jax.random.uniform(jax.random.fold_in(jax.random.fold_in(stream_key, 6), dim), (parts,), jnp.float32, least / len(cuts), largest / len(cuts))
        level = level * jnp.repeat(jnp.exp(draws), extent[dim] // parts).reshape((-1,) + (1,) * (len(extent) - 1 - dim))
    return level


def length_profile(number_of, total, reach, slope):
    loads = [(1 << 20) // math.isqrt(standing ** slope) + 1 for standing in range(2, number_of + 1)]
    rest, given = total - reach - (number_of - 1), [1] * (number_of - 1)
    while rest > 0:
        movable = [i for i in range(number_of - 1) if given[i] < reach]
        mass, remaining = sum([loads[i] for i in movable]), rest
        for i in movable:
            extra = min(reach - given[i], max(1, remaining * loads[i] // mass), rest)
            given[i] = given[i] + extra
            rest = rest - extra
    return np.array([reach] + given)


def uneven(stream_key, amount, total, reach, slope):
    if amount == 2:
        one = jax.random.randint(stream_key, (), max(1, total - reach), min(reach, total - 1) + 1)
        return jnp.stack([one, total - one])
    sizes = jnp.asarray(length_profile(amount, total, reach, slope), jnp.int32)
    pairs = (amount - 1) // 2
    giver, taker = sizes[1:1 + 2 * pairs:2], sizes[2:2 + 2 * pairs:2]
    margin = jnp.minimum(giver - 1, reach - taker)
    moved = jax.random.randint(jax.random.fold_in(stream_key, 1), (pairs,), 0, 1 << 20) % (margin + 1)
    sizes = sizes.at[1:1 + 2 * pairs:2].set(giver - moved).at[2:2 + 2 * pairs:2].set(taker + moved)
    return sizes[jax.random.permutation(jax.random.fold_in(stream_key, 2), amount)]


def centred(rng, shape, spread, limit, split=(), held_as=jnp.bfloat16):
    values = jax.random.normal(rng, shape, jnp.float32) * spread
    if len(split) > 0:
        values = block_scale(rng, shape, split, -0.22, 0.18) * values
    return jnp.clip(values, min=-limit, max=limit).astype(held_as)


def setup_inputs(seed: int = 0) -> dict:
    key_of = jax.random.split(jax.random.key(seed), 15)
    return {
        "residual_in": centred(key_of[0], (STREAM, D), 0.25, 2.5, ((0, 256),)),
        "queries": draw_queries(jax.random.fold_in(key_of[14], 71), 0),
        "fresh_pairs": draw_fresh_pairs(jax.random.fold_in(key_of[14], 71), 0),
        "cache_pairs": centred(key_of[3], (CACHE, 2 * KV_HEADS * HD), 1.0, 6.0, ((0, 32),)),
        "segment_ids": jnp.searchsorted(jnp.cumsum(uneven(key_of[4], SEGS, STREAM, SEG_MAX, 2)), jnp.arange(STREAM), side="right").astype(jnp.int32),
        "prefix_length": draw_prefix_length(jax.random.fold_in(key_of[14], 71), 0),
        "page_order": jax.random.permutation(key_of[6], NPAGES).astype(jnp.int32),
        "out_weight": centred(key_of[7], (HEADS * HD, D), (HEADS * HD) ** -0.5, 0.125, ((0, 8),)),
        "post_gain": jnp.clip(1.0 + 0.15 * jax.random.normal(key_of[8], (D,), jnp.float32), 0.25, 1.75),
        "gate_weight": centred(key_of[9], (D, FF), D ** -0.5, 0.125, ((1, 8),)),
        "up_weight": centred(key_of[10], (D, FF), D ** -0.5, 0.125, ((1, 8),)),
        "down_weight": centred(key_of[11], (FF, D), FF ** -0.5, 0.09375, ((0, 8),)),
        "next_gain": jnp.clip(1.0 + 0.15 * jax.random.normal(key_of[12], (D,), jnp.float32), 0.25, 1.75),
        "next_weight": centred(key_of[13], (D, (HEADS + 2 * KV_HEADS) * HD), D ** -0.5, 0.125, ((1, 8),)),
    }


masked_score = -1e+30
norm_epsilon = 1e-05

def page_tables(segment_ids, prefix_length, page_order, page_rows):
    seg_count = prefix_length.shape[0]
    seg_range = jnp.arange(seg_count, dtype=jnp.int32)
    seg_len = lax.optimization_barrier(jnp.sum((segment_ids[None, :] == seg_range[:, None]).astype(jnp.int32), axis=1, dtype=jnp.int32))
    seg_start = (jnp.cumsum(seg_len, dtype=jnp.int32) - seg_len).astype(jnp.int32)
    needed = ((prefix_length + seg_len + page_rows - 1) // page_rows).astype(jnp.int32)
    cum_end = jnp.cumsum(needed, dtype=jnp.int32)
    first_slot = (cum_end - needed).astype(jnp.int32)
    page_count = page_order.shape[0]
    page_range = jnp.arange(page_count, dtype=jnp.int32)
    ranking = lax.optimization_barrier(jnp.sum(jnp.where(page_order[None, :] == page_range[:, None], page_range[None, :], 0), axis=1, dtype=jnp.int32))
    owners = lax.optimization_barrier(jnp.sum((cum_end[None, :] <= ranking[:, None]).astype(jnp.int32), axis=1, dtype=jnp.int32))
    onehot = (owners[:, None] == seg_range[None, :]).astype(jnp.int32)
    page_first = ((ranking - lax.optimization_barrier(jnp.sum(onehot * first_slot[None, :], axis=1, dtype=jnp.int32))) * page_rows).astype(jnp.int32)
    page_prefix = lax.optimization_barrier(jnp.sum(onehot * prefix_length[None, :], axis=1, dtype=jnp.int32))
    page_len = lax.optimization_barrier(jnp.sum(onehot * seg_len[None, :], axis=1, dtype=jnp.int32))
    page_start = lax.optimization_barrier(jnp.sum(onehot * seg_start[None, :], axis=1, dtype=jnp.int32))
    return (seg_start, first_slot, owners, page_first, page_prefix, page_len, page_start)

def rms_scale(rows, gain):
    values = rows.astype(jnp.float32)
    scaled = values * lax.rsqrt(lax.optimization_barrier(jnp.mean(values * values, axis=-1, keepdims=True)) + norm_epsilon)
    return (scaled * gain.astype(jnp.float32)).astype(jnp.bfloat16)

def reference(residual_in, queries, fresh_pairs, cache_pairs, segment_ids, prefix_length, page_order, out_weight, post_gain, gate_weight, up_weight, down_weight, next_gain, next_weight):
    tables = page_tables(segment_ids, prefix_length, page_order, PAGE)
    seg_start, first_slot, owners, page_first, page_prefix, page_len, page_start = tables
    score_scale = 1.0 / math.sqrt(HD)
    seg_range = jnp.arange(SEGS, dtype=jnp.int32)
    place = jnp.arange(PREFIX_MAX, dtype=jnp.int32)
    slot = jnp.clip(first_slot[:, None] + place[None, :] // PAGE, 0, NPAGES - 1).astype(jnp.int32)
    pages = page_order[slot]
    prefix_rows = (pages * PAGE + place[None, :] % PAGE).reshape(-1).astype(jnp.int32)
    prefix_live = (place[None, :] < prefix_length[:, None]).reshape(-1)
    prefix_seg = jnp.repeat(seg_range, PREFIX_MAX)
    prefix_four = cache_pairs[prefix_rows].reshape(SEGS * PREFIX_MAX, KV_HEADS, 2, HD).astype(jnp.float32)
    fresh_four = fresh_pairs.reshape(STREAM, KV_HEADS, 2, HD)
    block_rows = min(256, STREAM // 2)
    window = min(STREAM, SEG_MAX + block_rows)

    def attend_block(index):
        block_first = (index * block_rows).astype(jnp.int32)
        query_block = lax.dynamic_slice_in_dim(queries, block_first, block_rows).reshape(block_rows, KV_HEADS, HEADS // KV_HEADS, HD).astype(jnp.float32)
        query_seg = lax.dynamic_slice_in_dim(segment_ids, block_first, block_rows)
        query_pos = block_first + jnp.arange(block_rows, dtype=jnp.int32)
        window_first = jnp.clip(block_first + block_rows - window, 0, STREAM - window).astype(jnp.int32)
        window_pairs = lax.dynamic_slice_in_dim(fresh_four, window_first, window).astype(jnp.float32)
        window_seg = lax.dynamic_slice_in_dim(segment_ids, window_first, window)
        window_pos = window_first + jnp.arange(window, dtype=jnp.int32)
        fresh_visible = (window_seg[None, :] == query_seg[:, None]) & (window_pos[None, :] <= query_pos[:, None])
        prefix_visible = (prefix_seg[None, :] == query_seg[:, None]) & prefix_live[None, :]
        fresh_live = fresh_visible[:, None, None, :]
        prefix_mask = prefix_visible[:, None, None, :]
        fresh_scores = jnp.einsum('bkgd,nkd->bkgn', query_block, window_pairs[:, :, 0]) * score_scale
        prefix_scores = jnp.einsum('bkgd,nkd->bkgn', query_block, prefix_four[:, :, 0]) * score_scale
        fresh_scores = jnp.where(fresh_live, fresh_scores, masked_score)
        prefix_scores = jnp.where(prefix_mask, prefix_scores, masked_score)
        peak = jnp.maximum(lax.optimization_barrier(jnp.max(fresh_scores, axis=3)), lax.optimization_barrier(jnp.max(prefix_scores, axis=3)))
        fresh_weights = jnp.where(fresh_live, jnp.exp(fresh_scores - peak[..., None]), 0.0)
        prefix_weights = jnp.where(prefix_mask, jnp.exp(prefix_scores - peak[..., None]), 0.0)
        totals = lax.optimization_barrier(jnp.sum(fresh_weights, axis=3)) + lax.optimization_barrier(jnp.sum(prefix_weights, axis=3))
        fresh_rounded = lax.optimization_barrier(fresh_weights.astype(jnp.bfloat16)).astype(jnp.float32)
        prefix_rounded = lax.optimization_barrier(prefix_weights.astype(jnp.bfloat16)).astype(jnp.float32)
        weighted = jnp.einsum('bkgn,nkd->bkgd', fresh_rounded, window_pairs[:, :, 1])
        weighted = weighted + jnp.einsum('bkgn,nkd->bkgd', prefix_rounded, prefix_four[:, :, 1])
        return (weighted / totals[..., None]).reshape(block_rows, HEADS * HD).astype(jnp.bfloat16)
    attended = lax.map(attend_block, jnp.arange(STREAM // block_rows, dtype=jnp.int32)).reshape(STREAM, HEADS * HD)
    row_pos = jnp.repeat(page_first, PAGE) + jnp.arange(CACHE, dtype=jnp.int32) % PAGE
    row_prefix = jnp.repeat(page_prefix, PAGE)
    row_len = jnp.repeat(page_len, PAGE)
    row_start = jnp.repeat(page_start, PAGE)
    write_live = (row_pos >= row_prefix) & (row_pos < row_prefix + row_len)
    write_token = jnp.clip(row_start + row_pos - row_prefix, 0, STREAM - 1).astype(jnp.int32)
    new_cache = jnp.where(write_live[:, None], fresh_pairs[write_token], cache_pairs)
    mixed = jnp.dot(attended, out_weight, preferred_element_type=jnp.float32)
    first_sum = (residual_in.astype(jnp.float32) + mixed).astype(jnp.bfloat16)
    post_normed = rms_scale(first_sum, post_gain)
    gate = jnp.dot(post_normed, gate_weight, preferred_element_type=jnp.float32)
    up_part = jnp.dot(post_normed, up_weight, preferred_element_type=jnp.float32)
    hidden = (jax.nn.silu(gate) * up_part).astype(jnp.bfloat16)
    ffn_out = jnp.dot(hidden, down_weight, preferred_element_type=jnp.float32)
    layer_out = (first_sum.astype(jnp.float32) + ffn_out).astype(jnp.bfloat16)
    next_normed = rms_scale(layer_out, next_gain)
    next_proj = jnp.dot(next_normed, next_weight, preferred_element_type=jnp.float32).astype(jnp.bfloat16)
    return (attended, new_cache, layer_out, next_proj)
```

```python
import functools
import math

import jax
import jax.numpy as jnp
from jax import lax
from jax.experimental import pallas as pl
from jax.experimental.pallas import tpu as pltpu
from jax.sharding import PartitionSpec as P

HD = 256
PAGE = 16
TILE = 256
MESH = pl.DeviceIdType.MESH
VMEM_LIMIT = 60 * 1024 * 1024

masked_score = -1e30
norm_epsilon = 1e-05


def page_tables(segment_ids, prefix_length, page_order, page_rows):
    seg_count = prefix_length.shape[0]
    seg_range = jnp.arange(seg_count, dtype=jnp.int32)
    seg_len = jnp.sum(
        (segment_ids[None, :] == seg_range[:, None]).astype(jnp.int32), axis=1, dtype=jnp.int32
    )
    seg_start = jnp.cumsum(seg_len, dtype=jnp.int32) - seg_len
    needed = (prefix_length + seg_len + page_rows - 1) // page_rows
    cum_end = jnp.cumsum(needed, dtype=jnp.int32)
    first_slot = cum_end - needed
    page_count = page_order.shape[0]
    page_range = jnp.arange(page_count, dtype=jnp.int32)
    ranking = jnp.sum(
        jnp.where(page_order[None, :] == page_range[:, None], page_range[None, :], 0),
        axis=1,
        dtype=jnp.int32,
    )
    owners = jnp.sum(
        (cum_end[None, :] <= ranking[:, None]).astype(jnp.int32), axis=1, dtype=jnp.int32
    )
    onehot = (owners[:, None] == seg_range[None, :]).astype(jnp.int32)
    page_first = (
        ranking - jnp.sum(onehot * first_slot[None, :], axis=1, dtype=jnp.int32)
    ) * page_rows
    page_prefix = jnp.sum(onehot * prefix_length[None, :], axis=1, dtype=jnp.int32)
    page_len = jnp.sum(onehot * seg_len[None, :], axis=1, dtype=jnp.int32)
    page_start = jnp.sum(onehot * seg_start[None, :], axis=1, dtype=jnp.int32)
    return seg_start, first_slot, (owners, page_first, page_prefix, page_len, page_start)


def row_info(tables, row_first, count, page_rows):
    sliced = [
        jnp.repeat(
            lax.dynamic_slice_in_dim(table, row_first // page_rows, count // page_rows), page_rows
        )
        for table in tables
    ]
    position = sliced[1] + (row_first + jnp.arange(count, dtype=jnp.int32)) % page_rows
    return (sliced[0], position, sliced[2], sliced[3], sliced[4])


def attend_kernel(
    pages_per_seg,
    info_ref,
    prefix_ref,
    rows_ref,
    q_ref,
    seg_ref,
    low_ref,
    fresh_ref,
    cache_ref,
    out_ref,
    tiles,
    prefix_tile,
    peak,
    total,
    acc,
    tile_sem,
    page_sem,
):
    first, last, seg_lo, seg_hi = info_ref[0], info_ref[1], info_ref[2], info_ref[3]
    rows = q_ref.shape[0]

    def tile_copy(index, slot):
        source = fresh_ref.at[pl.ds(pl.multiple_of(index * TILE, TILE), TILE), :]
        return pltpu.make_async_copy(source, tiles.at[slot], tile_sem.at[slot])

    def page_copy(seg, j):
        row = pl.multiple_of(rows_ref[seg * pages_per_seg + j], PAGE)
        source = cache_ref.at[pl.ds(row, PAGE), :]
        return pltpu.make_async_copy(
            source, prefix_tile.at[pl.ds(pl.multiple_of(j * PAGE, PAGE), PAGE), :], page_sem.at[j]
        )

    def pages_of(seg):
        return (prefix_ref[seg] + PAGE - 1) // PAGE

    tile_copy(first, 0).start()
    prefix_tile[...] = jnp.zeros_like(prefix_tile)
    peak[...] = jnp.full_like(peak, masked_score)
    total[...] = jnp.zeros_like(total)
    acc[...] = jnp.zeros_like(acc)
    row_at = last * TILE + lax.broadcasted_iota(jnp.int32, (rows, TILE), 0)
    column = lax.broadcasted_iota(jnp.int32, (rows, TILE), 1)
    scale = 1.0 / math.sqrt(HD)

    def absorb(keys, values, live):
        scores = lax.dot_general(
            q_ref[...], keys, (((1,), (1,)), ((), ())), preferred_element_type=jnp.float32
        )
        scores = jnp.where(live, scores * scale, masked_score)
        before = peak[...]
        raised = jnp.maximum(before, jnp.max(scores, axis=1, keepdims=True))
        weights = jnp.where(live, jnp.exp(scores - raised), 0.0)
        rescale = jnp.exp(before - raised)
        peak[...] = raised
        total[...] = total[...] * rescale + jnp.sum(weights, axis=1, keepdims=True)
        acc[...] = acc[...] * rescale + jnp.dot(
            weights.astype(jnp.bfloat16), values, preferred_element_type=jnp.float32
        )

    @pl.loop(first, last + 1)
    def _(index):
        slot = (index - first) % 2
        tile_copy(index, slot).wait()

        @pl.when(index < last)
        def _():
            tile_copy(index + 1, 1 - slot).start()

        key_at = index * TILE + column
        live = (key_at >= low_ref[...]) & (key_at <= row_at)
        absorb(tiles[slot, :, :HD], tiles[slot, :, HD:], live)

    @pl.loop(seg_lo, seg_hi + 1)
    def _(seg):
        count = pages_of(seg)

        @pl.loop(0, count)
        def _(j):
            page_copy(seg, j).start()

        @pl.loop(0, count)
        def _(j):
            page_copy(seg, j).wait()

        @pl.when(count > 0)
        def _():
            live = (seg_ref[...] == seg) & (column < prefix_ref[seg])
            absorb(prefix_tile[:, :HD], prefix_tile[:, HD:], live)

    out_ref[...] = (acc[...] / total[...]).astype(out_ref.dtype)


def attend(info, prefix_length, page_rows, queries, own_seg, own_low, fresh, cache):
    rows = queries.shape[0]
    pages_per_seg = page_rows.shape[0] // prefix_length.shape[0]
    smem = pl.BlockSpec(memory_space=pltpu.SMEM)
    vmem = pl.BlockSpec(memory_space=pltpu.VMEM)
    hbm = pl.BlockSpec(memory_space=pl.ANY)
    return pl.pallas_call(
        functools.partial(attend_kernel, pages_per_seg),
        out_shape=jax.ShapeDtypeStruct((rows, HD), jnp.bfloat16),
        in_specs=[smem, smem, smem, vmem, vmem, vmem, hbm, hbm],
        out_specs=vmem,
        scratch_shapes=[
            pltpu.VMEM((2, TILE, 2 * HD), jnp.bfloat16),
            pltpu.VMEM((pages_per_seg * PAGE, 2 * HD), jnp.bfloat16),
            pltpu.VMEM((rows, 1), jnp.float32),
            pltpu.VMEM((rows, 1), jnp.float32),
            pltpu.VMEM((rows, HD), jnp.float32),
            pltpu.SemaphoreType.DMA((2,)),
            pltpu.SemaphoreType.DMA((pages_per_seg,)),
        ],
        name="attend",
    )(info, prefix_length, page_rows, queries, own_seg, own_low, fresh, cache)


def chain_kernel(
    groups,
    attended_ref,
    residual_ref,
    post_gain_ref,
    next_gain_ref,
    wo_hbm,
    wg_hbm,
    wu_hbm,
    wd_hbm,
    wn_hbm,
    layer_ref,
    next_ref,
    wo,
    wg,
    wu,
    wd,
    wn,
    partial,
    hidden,
    sums,
    outgoing,
    incoming,
    gathered,
    weight_sem,
    sum_send,
    sum_recv,
    copy_send,
    copy_recv,
):
    me = lax.axis_index("grp")
    width = layer_ref.shape[1]
    chunk = layer_ref.shape[0]
    half = width // 2
    far = groups // 2
    steps = (1, -1)
    neighbour = [lax.rem(me + 1, groups), lax.rem(me + groups - 1, groups)]

    loads = []
    for i, (source, target) in enumerate(
        ((wo_hbm, wo), (wg_hbm, wg), (wu_hbm, wu), (wd_hbm, wd), (wn_hbm, wn))
    ):
        loads.append(pltpu.make_async_copy(source, target, weight_sem.at[i]))
        loads[i].start()

    barrier = pltpu.get_barrier_semaphore()
    for d in range(2):
        pl.semaphore_signal(
            barrier, inc=1, device_id={"grp": neighbour[d]}, device_id_type=MESH
        )
    pl.semaphore_wait(barrier, 2)

    def rows_of(owner):
        index = lax.rem(owner + 2 * groups, groups)
        return pl.ds(pl.multiple_of(index * chunk, chunk), chunk)

    def columns_of(h):
        return pl.ds(h * half, half)

    def sum_copy(phase, d, h, s):
        return pltpu.make_async_remote_copy(
            src_ref=outgoing.at[phase, d, h, s],
            dst_ref=incoming.at[phase, d, h, s],
            send_sem=sum_send.at[phase, d, h, s],
            recv_sem=sum_recv.at[phase, d, h, s],
            device_id={"grp": neighbour[d]},
            device_id_type=MESH,
        )

    def gather_copy(phase, d, h, k):
        block = gathered.at[phase, rows_of(me - steps[d] * k), columns_of(h)]
        return pltpu.make_async_remote_copy(
            src_ref=block,
            dst_ref=block,
            send_sem=copy_send.at[phase, d, h, k],
            recv_sem=copy_recv.at[phase, d, h, k],
            device_id={"grp": neighbour[d]},
            device_id_type=MESH,
        )

    def reduce_scatter(phase):
        for s in range(far):
            for h in range(2):
                for d in range(2):
                    first = 0 if h == d else 1
                    if s < first:
                        continue
                    owner = me + steps[d] * (far - s)
                    value = partial[rows_of(owner), columns_of(h)]
                    if s > first:
                        sum_copy(phase, d, h, s - 1).wait_recv()
                        value = value + incoming[phase, d, h, s - 1].astype(jnp.float32)
                    outgoing[phase, d, h, s] = value.astype(jnp.bfloat16)
                    sum_copy(phase, d, h, s).start()
        for h in range(2):
            value = partial[rows_of(me), columns_of(h)]
            for d in range(2):
                sum_copy(phase, d, h, far - 1).wait_recv()
                value = value + incoming[phase, d, h, far - 1].astype(jnp.float32)
            sums[:, columns_of(h)] = value
        for s in range(far):
            for h in range(2):
                for d in range(2):
                    if s >= (0 if h == d else 1):
                        sum_copy(phase, d, h, s).wait_send()

    def all_gather(phase):
        for k in range(far):
            for h in range(2):
                for d in range(2):
                    if k >= (far if h == d else far - 1):
                        continue
                    if k > 0:
                        gather_copy(phase, d, h, k - 1).wait_recv()
                    gather_copy(phase, d, h, k).start()
        for h in range(2):
            for d in range(2):
                gather_copy(phase, d, h, (far if h == d else far - 1) - 1).wait_recv()
        for k in range(far):
            for h in range(2):
                for d in range(2):
                    if k < (far if h == d else far - 1):
                        gather_copy(phase, d, h, k).wait_send()

    def normed(values, gain_ref):
        scaled = values * lax.rsqrt(
            jnp.mean(values * values, axis=-1, keepdims=True) + norm_epsilon
        )
        return (scaled * gain_ref[...]).astype(jnp.bfloat16)

    loads[0].wait()

    @pl.loop(0, width // 256)
    def _(j):
        columns = pl.ds(pl.multiple_of(j * 256, 256), 256)
        partial[:, columns] = jnp.dot(
            attended_ref[...], wo[:, columns], preferred_element_type=jnp.float32
        )

    reduce_scatter(0)
    first_sum = (residual_ref[...].astype(jnp.float32) + sums[...]).astype(jnp.bfloat16)
    layer_ref[...] = first_sum
    gathered[0, rows_of(me), :] = normed(first_sum.astype(jnp.float32), post_gain_ref)
    all_gather(0)

    loads[1].wait()
    loads[2].wait()

    @pl.loop(0, wg.shape[1] // 256)
    def _(j):
        columns = pl.ds(pl.multiple_of(j * 256, 256), 256)
        rows = gathered[0]
        gate = jnp.dot(rows, wg[:, columns], preferred_element_type=jnp.float32)
        up = jnp.dot(rows, wu[:, columns], preferred_element_type=jnp.float32)
        hidden[:, columns] = (jax.nn.silu(gate) * up).astype(jnp.bfloat16)

    loads[3].wait()

    @pl.loop(0, width // 256)
    def _(j):
        columns = pl.ds(pl.multiple_of(j * 256, 256), 256)
        partial[:, columns] = jnp.dot(
            hidden[...], wd[:, columns], preferred_element_type=jnp.float32
        )

    reduce_scatter(1)
    layer_out = (layer_ref[...].astype(jnp.float32) + sums[...]).astype(jnp.bfloat16)
    layer_ref[...] = layer_out
    gathered[1, rows_of(me), :] = normed(layer_out.astype(jnp.float32), next_gain_ref)
    all_gather(1)

    loads[4].wait()

    @pl.loop(0, wn.shape[1] // 256)
    def _(j):
        columns = pl.ds(pl.multiple_of(j * 256, 256), 256)
        next_ref[:, columns] = jnp.dot(
            gathered[1], wn[:, columns], preferred_element_type=jnp.float32
        ).astype(jnp.bfloat16)


def chain(attended, residual, post_gain, next_gain, wo, wg, wu, wd, wn, groups):
    rows = attended.shape[0]
    chunk, width = residual.shape
    far = groups // 2
    vmem = pl.BlockSpec(memory_space=pltpu.VMEM)
    hbm = pl.BlockSpec(memory_space=pl.ANY)
    messages = (2, 2, 2, far)
    return pl.pallas_call(
        functools.partial(chain_kernel, groups),
        out_shape=(
            jax.ShapeDtypeStruct((chunk, width), jnp.bfloat16),
            jax.ShapeDtypeStruct((rows, wn.shape[1]), jnp.bfloat16),
        ),
        in_specs=[vmem] * 4 + [hbm] * 5,
        out_specs=(vmem, vmem),
        scratch_shapes=[pltpu.VMEM(w.shape, w.dtype) for w in (wo, wg, wu, wd, wn)]
        + [
            pltpu.VMEM((rows, width), jnp.float32),
            pltpu.VMEM((rows, wg.shape[1]), jnp.bfloat16),
            pltpu.VMEM((chunk, width), jnp.float32),
            pltpu.VMEM(messages + (chunk, width // 2), jnp.bfloat16),
            pltpu.VMEM(messages + (chunk, width // 2), jnp.bfloat16),
            pltpu.VMEM((2, rows, width), jnp.bfloat16),
            pltpu.SemaphoreType.DMA((5,)),
            pltpu.SemaphoreType.DMA(messages),
            pltpu.SemaphoreType.DMA(messages),
            pltpu.SemaphoreType.DMA(messages),
            pltpu.SemaphoreType.DMA(messages),
        ],
        compiler_params=pltpu.CompilerParams(
            collective_id=1, has_side_effects=True, vmem_limit_bytes=VMEM_LIMIT
        ),
        name="chain",
    )(attended, residual, post_gain, next_gain, wo, wg, wu, wd, wn)


def local(
    residual_in,
    queries,
    fresh_pairs,
    cache_pairs,
    segment_ids,
    prefix_length,
    page_order,
    out_weight,
    post_gain,
    gate_weight,
    up_weight,
    down_weight,
    next_gain,
    next_weight,
):
    group = lax.axis_index("grp")
    shard = lax.axis_index("tok")
    groups = lax.axis_size("grp")
    tok_rows = queries.shape[0]
    kv_first = group // 2
    width_pairs = 2 * HD
    own_cols = cache_pairs.shape[1] // groups
    own_offset = group * own_cols - kv_first * width_pairs
    own_first = shard * tok_rows
    own_seg = lax.dynamic_slice_in_dim(segment_ids, own_first, tok_rows)
    seg_start, first_slot, tables = page_tables(segment_ids, prefix_length, page_order, PAGE)
    cache_rows = cache_pairs.shape[0]
    cache_first = shard * cache_rows
    fresh_mine = lax.dynamic_slice_in_dim(fresh_pairs, kv_first * width_pairs, width_pairs, 1)
    cache_mine = lax.dynamic_slice_in_dim(cache_pairs, kv_first * width_pairs, width_pairs, 1)
    fresh_all = lax.all_gather(fresh_mine, "tok", axis=0, tiled=True)
    cache_all = lax.all_gather(cache_mine, "tok", axis=0, tiled=True)

    seg_range = jnp.arange(prefix_length.shape[0], dtype=jnp.int32)
    own_low = jnp.sum(
        jnp.where(own_seg[:, None] == seg_range[None, :], seg_start[None, :], 0), axis=1
    )
    info = jnp.stack([own_low[0] // TILE, shard * tok_rows // TILE, own_seg[0], own_seg[-1]])
    most_pages = 256 // PAGE
    slots = jnp.clip(
        first_slot[:, None] + jnp.arange(most_pages, dtype=jnp.int32)[None, :],
        0,
        page_order.shape[0] - 1,
    )
    page_rows = (page_order[slots] * PAGE).reshape(-1)
    attended = attend(
        info,
        prefix_length,
        page_rows,
        queries,
        own_seg[:, None],
        own_low[:, None],
        fresh_all,
        cache_all,
    )

    cache_info = row_info(tables, cache_first, cache_rows, PAGE)
    write_live = (cache_info[1] >= cache_info[2]) & (cache_info[1] < cache_info[2] + cache_info[3])
    write_token = cache_info[4] + cache_info[1] - cache_info[2]
    own_cache = lax.dynamic_slice_in_dim(cache_pairs, group * own_cols, own_cols, 1)
    mine = lax.dynamic_slice_in_dim(fresh_all, own_offset, own_cols, 1)
    taken = jnp.take(mine, jnp.clip(write_token, 0, fresh_all.shape[0] - 1), axis=0)
    written = jnp.where(write_live[:, None], taken, own_cache)

    layer_out, next_proj = chain(
        attended,
        residual_in,
        post_gain[None, :],
        next_gain[None, :],
        out_weight,
        gate_weight,
        up_weight,
        down_weight,
        next_weight,
        groups,
    )
    return (attended, written, layer_out, next_proj)


def solution(mesh):
    in_specs = (
        P(("tok", "grp"), None),
        P("tok", "grp"),
        P("tok", None),
        P("tok", None),
        P(),
        P(),
        P(),
        P("grp", None),
        P(),
        P(None, "grp"),
        P(None, "grp"),
        P("grp", None),
        P(),
        P(None, "grp"),
    )
    out_specs = (P("tok", "grp"), P("tok", "grp"), P(("tok", "grp"), None), P("tok", "grp"))
    return jax.shard_map(local, mesh=mesh, in_specs=in_specs, out_specs=out_specs, check_vma=False)
```

```python
import functools
import math

import jax
import jax.numpy as jnp
from jax import lax
from jax.experimental import pallas as pl
from jax.experimental.pallas import tpu as pltpu
from jax.sharding import PartitionSpec as P

HD = 256
PAGE = 16
TILE = 256
MESH = pl.DeviceIdType.MESH
VMEM_LIMIT = 60 * 1024 * 1024
FEW_PAGES = 12

masked_score = -1e30
lowest_peak = -1e20
norm_epsilon = 1e-05

START, LENGTH, SLOT, WHERE, SLOTS, COUNTS, MOST, TABLES = 0, 16, 32, 64, 320, 384, 448, 512

smem = pl.BlockSpec(memory_space=pltpu.SMEM)
vmem = pl.BlockSpec(memory_space=pltpu.VMEM)
hbm = pl.BlockSpec(memory_space=pl.ANY)


def pack_kernel(
    shards,
    ids_ref,
    order_block_ref,
    prefix_ref,
    order_ref,
    fresh_ref,
    cache_ref,
    key_tile,
    value_tile,
    tables,
    tile_sem,
    page_sem,
):
    shard, group = lax.axis_index("tok"), lax.axis_index("grp")
    own_pages = order_ref.shape[0] // shards
    seg_count = prefix_ref.shape[0]
    pairs_at = (group // 2) * 2 * HD
    targets = (key_tile, value_tile)

    def columns(part):
        return pl.ds(pl.multiple_of(pairs_at + part * HD, HD), HD)

    def fresh_copy(part):
        return pltpu.make_async_copy(
            fresh_ref.at[:, columns(part)],
            targets[part].at[pl.ds(0, TILE), :],
            tile_sem.at[part],
        )

    def page_copy(page, rank, part):
        return pltpu.make_async_copy(
            cache_ref.at[pl.ds(pl.multiple_of(page * PAGE, PAGE), PAGE), columns(part)],
            targets[part].at[pl.ds(pl.multiple_of(TILE + rank * PAGE, PAGE), PAGE), :],
            page_sem.at[rank, part],
        )

    for part in range(2):
        fresh_copy(part).start()

    ids = ids_ref[...]
    starts = [jnp.int32(0)]
    for s in range(1, seg_count):
        starts.append(jnp.sum((ids < s).astype(jnp.float32)).astype(jnp.int32))
    starts.append(jnp.int32(ids_ref.shape[0] * ids_ref.shape[1]))
    slot = jnp.int32(0)
    for s in range(seg_count):
        length = starts[s + 1] - starts[s]
        tables[START + s] = starts[s]
        tables[LENGTH + s] = length
        tables[SLOT + s] = slot
        slot = slot + (prefix_ref[s] + length + PAGE - 1) // PAGE
    tables[SLOT + seg_count] = slot

    for owner in range(shards):
        tables[COUNTS + owner] = 0
    tables[MOST] = 0

    @pl.loop(0, seg_count)
    def _(s):
        first = tables[SLOT + s]

        @pl.loop(0, (prefix_ref[s] + PAGE - 1) // PAGE)
        def _(j):
            page = order_ref[first + j]
            owner = page // own_pages
            rank = tables[COUNTS + owner]
            tables[COUNTS + owner] = rank + 1
            tables[MOST] = jnp.maximum(tables[MOST], rank + 1)
            tables[WHERE + s * PAGE + j] = owner * own_pages + rank

            @pl.when(owner == shard)
            def _():
                for part in range(2):
                    page_copy(page - owner * own_pages, rank, part).start()

    order = order_block_ref[...]
    at = lax.broadcasted_iota(jnp.int32, order.shape, 0) * order.shape[1] + (
        lax.broadcasted_iota(jnp.int32, order.shape, 1)
    )
    at = at.astype(jnp.float32)
    for i in range(own_pages):
        mine = order == shard * own_pages + i
        tables[SLOTS + i] = jnp.sum(jnp.where(mine, at, 0.0)).astype(jnp.int32)

    @pl.loop(0, tables[COUNTS + shard])
    def _(rank):
        for part in range(2):
            page_copy(0, rank, part).wait()

    for part in range(2):
        fresh_copy(part).wait()


def pack(segment_ids, prefix_length, page_order, fresh, cache, shards):
    own_pages = page_order.shape[0] // shards
    tile = jax.ShapeDtypeStruct((TILE + own_pages * PAGE, HD), jnp.bfloat16)
    return pl.pallas_call(
        functools.partial(pack_kernel, shards),
        out_shape=(tile, tile, jax.ShapeDtypeStruct((TABLES,), jnp.int32)),
        in_specs=[vmem, vmem, smem, smem, hbm, hbm],
        out_specs=(vmem, vmem, smem),
        scratch_shapes=[
            pltpu.SemaphoreType.DMA((2,)),
            pltpu.SemaphoreType.DMA((own_pages, 2)),
        ],
        name="pack",
    )(
        segment_ids.reshape(-1, 128),
        page_order.reshape(-1, 128),
        prefix_length,
        page_order,
        fresh,
        cache,
    )


SIDE = 4
ROUTES = {
    (0, 0): ("p+", "p-", "q+", "q-", "core"),
    (3, 0): ("q+", "q-", "p+", "core"),
    (1, 0): ("q+", "q-", "core"),
    (0, 3): ("q+", "core"),
    (0, 1): ("core",),
    (2, 0): ("q+", "q-", "core"),
    (3, 3): ("q+", "core"),
    (3, 1): ("core",),
    (1, 3): ("core",),
    (1, 1): ("q-", "core"),
    (0, 2): ("core",),
    (2, 3): ("core",),
    (2, 1): ("q-", "core"),
    (3, 2): ("core",),
    (1, 2): ("core",),
    (2, 2): ("core",),
}
MOVES = {"p+": (1, 0), "p-": (-1, 0), "q+": (0, 1), "q-": (0, -1), "core": (0, 0)}
MESSAGES = [(tile, way) for tile, ways in ROUTES.items() for way in ways]


def arrival(tile):
    for index, (sent, way) in enumerate(MESSAGES):
        move = MOVES[way]
        if way != "core" and ((sent[0] - move[0]) % SIDE, (sent[1] - move[1]) % SIDE) == tile:
            return index
    return None


def spread_kernel(rows, key_ref, value_ref, keys, values, own, send_sem, recv_sem, own_sem):
    shard = lax.axis_index("tok")
    core, x, y = shard % 2, (shard // 2) % SIDE, shard // (2 * SIDE)

    def shard_at(dx, dy, c):
        return (((y + dy + SIDE) % SIDE) * SIDE + (x + dx + SIDE) % SIDE) * 2 + c

    def place(part, p, q, c):
        return shard_at(p, q, c) if part == 0 else shard_at(q, p, c)

    sources, targets = (key_ref, value_ref), (keys, values)

    def message(part, index):
        tile, way = MESSAGES[index]
        move = MOVES[way]
        target = place(part, move[0], move[1], 1 - core if way == "core" else core)
        block = targets[part].at[place(part, tile[0], tile[1], core)]
        source = sources[part].at[pl.ds(0, rows), :] if tile == (0, 0) else block
        return pltpu.make_async_remote_copy(
            src_ref=source,
            dst_ref=block,
            send_sem=send_sem.at[part, index],
            recv_sem=recv_sem.at[part, index],
            device_id={"tok": target},
            device_id_type=MESH,
        )

    def fetch(part):
        return pltpu.make_async_copy(
            sources[part].at[pl.ds(0, rows), :], own.at[part], own_sem.at[part]
        )

    def store(part):
        return pltpu.make_async_copy(own.at[part], targets[part].at[shard], own_sem.at[part])

    barrier = pltpu.get_barrier_semaphore()
    peers = [shard_at(1, 0, core), shard_at(-1, 0, core), shard_at(0, 1, core)]
    peers += [shard_at(0, -1, core), shard_at(0, 0, 1 - core)]
    for peer in peers:
        pl.semaphore_signal(barrier, inc=1, device_id={"tok": peer}, device_id_type=MESH)
    for part in range(2):
        fetch(part).start()
    pl.semaphore_wait(barrier, len(peers))

    for tile in ROUTES:
        sent = [i for i, (t, _) in enumerate(MESSAGES) if t == tile]
        for part in range(2):
            if tile != (0, 0):
                message(part, arrival(tile)).wait_recv()
            for i in sent:
                message(part, i).start()
    for part in range(2):
        fetch(part).wait()
        store(part).start()
    for part in range(2):
        store(part).wait()
    for part in range(2):
        for i, (_, way) in enumerate(MESSAGES):
            if way == "core":
                message(part, i).wait_recv()
    for part in range(2):
        for i in range(len(MESSAGES)):
            message(part, i).wait_send()


def spread(key_tile, value_tile, rows, shards, collective_id):
    tiles = jax.ShapeDtypeStruct((shards, rows, HD), jnp.bfloat16)
    return pl.pallas_call(
        functools.partial(spread_kernel, rows),
        out_shape=(tiles, tiles),
        in_specs=[hbm, hbm],
        out_specs=(hbm, hbm),
        scratch_shapes=[
            pltpu.VMEM((2, rows, HD), jnp.bfloat16),
            pltpu.SemaphoreType.DMA((2, len(MESSAGES))),
            pltpu.SemaphoreType.DMA((2, len(MESSAGES))),
            pltpu.SemaphoreType.DMA((2,)),
        ],
        compiler_params=pltpu.CompilerParams(collective_id=collective_id, has_side_effects=True),
        name="spread",
    )(key_tile, value_tile)


def attend_kernel(
    seg_count,
    tables,
    prefix_ref,
    q_ref,
    keys_ref,
    values_ref,
    cache_ref,
    out_ref,
    written_ref,
    key_tiles,
    value_tiles,
    prefix_keys,
    prefix_values,
    windows,
    query,
    peak,
    total,
    acc,
    tile_sem,
    page_sem,
    window_sem,
    cache_sem,
):
    shard, group = lax.axis_index("tok"), lax.axis_index("grp")
    rows = q_ref.shape[0]
    own_pages = written_ref.shape[0] // PAGE
    shards = keys_ref.shape[0]
    sources = (keys_ref, values_ref)
    tiles = (key_tiles, value_tiles)
    prefixes = (prefix_keys, prefix_values)
    wide = 2 * TILE

    def cache_copy():
        columns = pl.ds(pl.multiple_of(group * HD, HD), HD)
        return pltpu.make_async_copy(cache_ref.at[:, columns], written_ref, cache_sem)

    def page_place(i):
        slot = tables[SLOTS + i]
        seg = jnp.int32(-1)
        for s in range(seg_count):
            seg = seg + (tables[SLOT + s] <= slot).astype(jnp.int32)
        position = (slot - tables[SLOT + seg]) * PAGE
        return seg, position, tables[START + seg] + position - prefix_ref[seg]

    def window_copy(part, i, side, block):
        block = jnp.clip(block, 0, shards * (TILE // PAGE) - 1)
        tile, row = block // (TILE // PAGE), (block % (TILE // PAGE)) * PAGE
        return pltpu.make_async_copy(
            sources[part].at[tile, pl.ds(pl.multiple_of(row, PAGE), PAGE), :],
            windows.at[i, pl.ds(side * PAGE, PAGE), :],
            window_sem.at[i, side],
        )

    def tile_copy(index, slot, side, part):
        return pltpu.make_async_copy(
            sources[part].at[jnp.maximum(index, 0), pl.ds(0, TILE), :],
            tiles[part].at[slot, pl.ds(side * TILE, TILE), :],
            tile_sem.at[slot, side, part],
        )

    def page_copy(seg, j, part):
        place = tables[WHERE + seg * PAGE + j]
        row = TILE + (place % own_pages) * PAGE
        return pltpu.make_async_copy(
            sources[part].at[place // own_pages, pl.ds(pl.multiple_of(row, PAGE), PAGE), :],
            prefixes[part].at[pl.ds(pl.multiple_of(j * PAGE, PAGE), PAGE), :],
            page_sem.at[j, part],
        )

    first_row = shard * rows
    seg_lo = jnp.int32(-1)
    seg_hi = jnp.int32(-1)
    for s in range(seg_count):
        seg_lo = seg_lo + (tables[START + s] <= first_row).astype(jnp.int32)
        seg_hi = seg_hi + (tables[START + s] <= first_row + rows - 1).astype(jnp.int32)
    first_tile = tables[START + seg_lo] // TILE
    last_low = tables[START + seg_hi]
    steps = (shard - first_tile) // 2 + 1
    base = shard + 1 - 2 * steps

    def start_tiles(step):
        for side in range(2):
            for part in range(2):
                tile_copy(base + 2 * step + side, step % 2, side, part).start()

    start_tiles(0)
    cache_copy().start()

    @pl.loop(0, own_pages)
    def _(i):
        _, _, token = page_place(i)
        block = (token + wide * PAGE) // PAGE - wide
        for part in range(2):

            @pl.when(group % 2 == part)
            def _():
                for side in range(2):
                    window_copy(part, i, side, block + side).start()

    for part in range(2):
        prefixes[part][...] = jnp.zeros_like(prefixes[part])
    peak[...] = jnp.full_like(peak, lowest_peak)
    total[...] = jnp.zeros_like(total)
    acc[...] = jnp.zeros_like(acc)
    query[...] = (q_ref[...].astype(jnp.float32) * (1.0 / math.sqrt(HD))).astype(jnp.bfloat16)
    row_at = first_row + lax.broadcasted_iota(jnp.int32, (rows, 1), 0)
    low = jnp.zeros((rows, 1), jnp.int32)
    seg_at = jnp.full((rows, 1), -1, jnp.int32)
    for s in range(seg_count):
        begun = row_at >= tables[START + s]
        low = jnp.where(begun, tables[START + s], low)
        seg_at = seg_at + begun.astype(jnp.int32)

    def absorb(keys, values, live):
        scores = lax.dot_general(
            query[...], keys, (((1,), (1,)), ((), ())), preferred_element_type=jnp.float32
        )
        if live is not None:
            scores = jnp.where(live, scores, masked_score)
        before = peak[...]
        raised = jnp.maximum(before, jnp.max(scores, axis=1, keepdims=True))
        weights = jnp.exp(scores - raised)
        rescale = jnp.exp(before - raised)
        peak[...] = raised
        total[...] = total[...] * rescale + jnp.sum(weights, axis=1, keepdims=True)
        acc[...] = acc[...] * rescale + jnp.dot(
            weights.astype(jnp.bfloat16), values, preferred_element_type=jnp.float32
        )

    @pl.loop(0, steps)
    def _(step):
        slot = step % 2
        for side in range(2):
            for part in range(2):
                tile_copy(base + 2 * step + side, slot, side, part).wait()

        @pl.when(step + 1 < steps)
        def _():
            start_tiles(step + 1)

        at = (base + 2 * step) * TILE
        whole = (at >= last_low) & (step + 1 < steps)

        @pl.when(whole)
        def _():
            absorb(key_tiles[slot], value_tiles[slot], None)

        @pl.when(jnp.logical_not(whole))
        def _():
            key_at = at + lax.broadcasted_iota(jnp.int32, (rows, wide), 1)
            absorb(key_tiles[slot], value_tiles[slot], (key_at >= low) & (key_at <= row_at))

    @pl.loop(seg_lo, seg_hi + 1)
    def _(seg):
        count = (prefix_ref[seg] + PAGE - 1) // PAGE

        @pl.loop(0, count)
        def _(j):
            for part in range(2):
                page_copy(seg, j, part).start()

        @pl.loop(0, count)
        def _(j):
            for part in range(2):
                page_copy(seg, j, part).wait()

        @pl.when(count > 0)
        def _():
            at = lax.broadcasted_iota(jnp.int32, (rows, prefix_keys.shape[0]), 1)
            absorb(prefix_keys[...], prefix_values[...], (seg_at == seg) & (at < prefix_ref[seg]))

    out_ref[...] = (acc[...] / total[...]).astype(out_ref.dtype)

    cache_copy().wait()

    @pl.loop(0, own_pages)
    def _(i):
        seg, position, token = page_place(i)
        for side in range(2):
            window_copy(0, i, side, 0).wait()
        shift = (token + wide * PAGE) % PAGE
        line = lax.broadcasted_iota(jnp.int32, (PAGE, 2 * PAGE), 0)
        taken = lax.broadcasted_iota(jnp.int32, (PAGE, 2 * PAGE), 1)
        picked = (taken == line + shift).astype(jnp.bfloat16)
        fresh = jnp.dot(picked, windows[i], preferred_element_type=jnp.float32)
        at = position + lax.broadcasted_iota(jnp.int32, (PAGE, HD), 0)
        used = tables[SLOTS + i] < tables[SLOT + seg_count]
        live = (at >= prefix_ref[seg]) & (at < prefix_ref[seg] + tables[LENGTH + seg]) & used
        block = pl.ds(pl.multiple_of(i * PAGE, PAGE), PAGE)
        held = written_ref[block, :].astype(jnp.float32)
        written_ref[block, :] = jnp.where(live, fresh, held).astype(jnp.bfloat16)


def attend(tables, prefix_length, queries, keys, values, cache):
    rows = queries.shape[0]
    most = 256
    own_pages = cache.shape[0] // PAGE
    return pl.pallas_call(
        functools.partial(attend_kernel, prefix_length.shape[0]),
        out_shape=(
            jax.ShapeDtypeStruct((rows, HD), jnp.bfloat16),
            jax.ShapeDtypeStruct((cache.shape[0], HD), jnp.bfloat16),
        ),
        in_specs=[smem, smem, vmem, hbm, hbm, hbm],
        out_specs=(vmem, vmem),
        scratch_shapes=[
            pltpu.VMEM((2, 2 * TILE, HD), jnp.bfloat16),
            pltpu.VMEM((2, 2 * TILE, HD), jnp.bfloat16),
            pltpu.VMEM((most, HD), jnp.bfloat16),
            pltpu.VMEM((most, HD), jnp.bfloat16),
            pltpu.VMEM((own_pages, 2 * PAGE, HD), jnp.bfloat16),
            pltpu.VMEM((rows, HD), jnp.bfloat16),
            pltpu.VMEM((rows, 1), jnp.float32),
            pltpu.VMEM((rows, 1), jnp.float32),
            pltpu.VMEM((rows, HD), jnp.float32),
            pltpu.SemaphoreType.DMA((2, 2, 2)),
            pltpu.SemaphoreType.DMA((most // PAGE, 2)),
            pltpu.SemaphoreType.DMA((own_pages, 2)),
            pltpu.SemaphoreType.DMA(()),
        ],
        name="attend",
    )(tables, prefix_length, queries, keys, values, cache)


def chain_kernel(
    groups,
    attended_ref,
    residual_ref,
    post_gain_ref,
    next_gain_ref,
    wo_hbm,
    wg_hbm,
    wu_hbm,
    wd_hbm,
    wn_hbm,
    layer_ref,
    next_ref,
    wo,
    wg,
    wu,
    wd,
    wn,
    partial,
    hidden,
    sums,
    outgoing,
    incoming,
    gathered,
    weight_sem,
    sum_send,
    sum_recv,
    copy_send,
    copy_recv,
):
    me = lax.axis_index("grp")
    width = layer_ref.shape[1]
    chunk = layer_ref.shape[0]
    half = width // 2
    far = groups // 2
    steps = (1, -1)
    neighbour = [lax.rem(me + 1, groups), lax.rem(me + groups - 1, groups)]

    loads = []
    for i, (source, target) in enumerate(
        ((wo_hbm, wo), (wg_hbm, wg), (wu_hbm, wu), (wd_hbm, wd), (wn_hbm, wn))
    ):
        loads.append(pltpu.make_async_copy(source, target, weight_sem.at[i]))
        loads[i].start()

    barrier = pltpu.get_barrier_semaphore()
    for d in range(2):
        pl.semaphore_signal(
            barrier, inc=1, device_id={"grp": neighbour[d]}, device_id_type=MESH
        )
    pl.semaphore_wait(barrier, 2)

    def rows_of(owner):
        index = lax.rem(owner + 2 * groups, groups)
        return pl.ds(pl.multiple_of(index * chunk, chunk), chunk)

    def columns_of(h):
        return pl.ds(h * half, half)

    def sum_copy(phase, d, h, s):
        return pltpu.make_async_remote_copy(
            src_ref=outgoing.at[phase, d, h, s],
            dst_ref=incoming.at[phase, d, h, s],
            send_sem=sum_send.at[phase, d, h, s],
            recv_sem=sum_recv.at[phase, d, h, s],
            device_id={"grp": neighbour[d]},
            device_id_type=MESH,
        )

    def gather_copy(phase, d, h, k):
        block = gathered.at[phase, rows_of(me - steps[d] * k), columns_of(h)]
        return pltpu.make_async_remote_copy(
            src_ref=block,
            dst_ref=block,
            send_sem=copy_send.at[phase, d, h, k],
            recv_sem=copy_recv.at[phase, d, h, k],
            device_id={"grp": neighbour[d]},
            device_id_type=MESH,
        )

    def reduce_scatter(phase):
        for s in range(far):
            for h in range(2):
                for d in range(2):
                    first = 0 if h == d else 1
                    if s < first:
                        continue
                    owner = me + steps[d] * (far - s)
                    value = partial[rows_of(owner), columns_of(h)]
                    if s > first:
                        sum_copy(phase, d, h, s - 1).wait_recv()
                        value = value + incoming[phase, d, h, s - 1].astype(jnp.float32)
                    outgoing[phase, d, h, s] = value.astype(jnp.bfloat16)
                    sum_copy(phase, d, h, s).start()
        for h in range(2):
            value = partial[rows_of(me), columns_of(h)]
            for d in range(2):
                sum_copy(phase, d, h, far - 1).wait_recv()
                value = value + incoming[phase, d, h, far - 1].astype(jnp.float32)
            sums[:, columns_of(h)] = value
        for s in range(far):
            for h in range(2):
                for d in range(2):
                    if s >= (0 if h == d else 1):
                        sum_copy(phase, d, h, s).wait_send()

    def all_gather(phase):
        for k in range(far):
            for h in range(2):
                for d in range(2):
                    if k >= (far if h == d else far - 1):
                        continue
                    if k > 0:
                        gather_copy(phase, d, h, k - 1).wait_recv()
                    gather_copy(phase, d, h, k).start()
        for h in range(2):
            for d in range(2):
                gather_copy(phase, d, h, (far if h == d else far - 1) - 1).wait_recv()
        for k in range(far):
            for h in range(2):
                for d in range(2):
                    if k < (far if h == d else far - 1):
                        gather_copy(phase, d, h, k).wait_send()

    def normed(values, gain_ref):
        scaled = values * lax.rsqrt(
            jnp.mean(values * values, axis=-1, keepdims=True) + norm_epsilon
        )
        return (scaled * gain_ref[...]).astype(jnp.bfloat16)

    loads[0].wait()

    @pl.loop(0, width // 256)
    def _(j):
        columns = pl.ds(pl.multiple_of(j * 256, 256), 256)
        partial[:, columns] = jnp.dot(
            attended_ref[...], wo[:, columns], preferred_element_type=jnp.float32
        )

    reduce_scatter(0)
    first_sum = (residual_ref[...].astype(jnp.float32) + sums[...]).astype(jnp.bfloat16)
    layer_ref[...] = first_sum
    gathered[0, rows_of(me), :] = normed(first_sum.astype(jnp.float32), post_gain_ref)
    all_gather(0)

    loads[1].wait()
    loads[2].wait()

    @pl.loop(0, wg.shape[1] // 256)
    def _(j):
        columns = pl.ds(pl.multiple_of(j * 256, 256), 256)
        rows = gathered[0]
        gate = jnp.dot(rows, wg[:, columns], preferred_element_type=jnp.float32)
        up = jnp.dot(rows, wu[:, columns], preferred_element_type=jnp.float32)
        hidden[:, columns] = (jax.nn.silu(gate) * up).astype(jnp.bfloat16)

    loads[3].wait()

    @pl.loop(0, width // 256)
    def _(j):
        columns = pl.ds(pl.multiple_of(j * 256, 256), 256)
        partial[:, columns] = jnp.dot(
            hidden[...], wd[:, columns], preferred_element_type=jnp.float32
        )

    reduce_scatter(1)
    layer_out = (layer_ref[...].astype(jnp.float32) + sums[...]).astype(jnp.bfloat16)
    layer_ref[...] = layer_out
    gathered[1, rows_of(me), :] = normed(layer_out.astype(jnp.float32), next_gain_ref)
    all_gather(1)

    loads[4].wait()

    @pl.loop(0, wn.shape[1] // 256)
    def _(j):
        columns = pl.ds(pl.multiple_of(j * 256, 256), 256)
        next_ref[:, columns] = jnp.dot(
            gathered[1], wn[:, columns], preferred_element_type=jnp.float32
        ).astype(jnp.bfloat16)


def chain(attended, residual, post_gain, next_gain, wo, wg, wu, wd, wn, groups):
    rows = attended.shape[0]
    chunk, width = residual.shape
    far = groups // 2
    vmem = pl.BlockSpec(memory_space=pltpu.VMEM)
    hbm = pl.BlockSpec(memory_space=pl.ANY)
    messages = (2, 2, 2, far)
    return pl.pallas_call(
        functools.partial(chain_kernel, groups),
        out_shape=(
            jax.ShapeDtypeStruct((chunk, width), jnp.bfloat16),
            jax.ShapeDtypeStruct((rows, wn.shape[1]), jnp.bfloat16),
        ),
        in_specs=[vmem] * 4 + [hbm] * 5,
        out_specs=(vmem, vmem),
        scratch_shapes=[pltpu.VMEM(w.shape, w.dtype) for w in (wo, wg, wu, wd, wn)]
        + [
            pltpu.VMEM((rows, width), jnp.float32),
            pltpu.VMEM((rows, wg.shape[1]), jnp.bfloat16),
            pltpu.VMEM((chunk, width), jnp.float32),
            pltpu.VMEM(messages + (chunk, width // 2), jnp.bfloat16),
            pltpu.VMEM(messages + (chunk, width // 2), jnp.bfloat16),
            pltpu.VMEM((2, rows, width), jnp.bfloat16),
            pltpu.SemaphoreType.DMA((5,)),
            pltpu.SemaphoreType.DMA(messages),
            pltpu.SemaphoreType.DMA(messages),
            pltpu.SemaphoreType.DMA(messages),
            pltpu.SemaphoreType.DMA(messages),
        ],
        compiler_params=pltpu.CompilerParams(
            collective_id=1, has_side_effects=True, vmem_limit_bytes=VMEM_LIMIT
        ),
        name="chain",
    )(attended, residual, post_gain, next_gain, wo, wg, wu, wd, wn)


def local(
    residual_in,
    queries,
    fresh_pairs,
    cache_pairs,
    segment_ids,
    prefix_length,
    page_order,
    out_weight,
    post_gain,
    gate_weight,
    up_weight,
    down_weight,
    next_gain,
    next_weight,
):
    groups, shards = lax.axis_size("grp"), lax.axis_size("tok")
    own_pages = page_order.shape[0] // shards
    key_tile, value_tile, tables = pack(
        segment_ids, prefix_length, page_order, fresh_pairs, cache_pairs, shards
    )

    def attention(pages, collective_id):
        keys, values = spread(key_tile, value_tile, TILE + pages * PAGE, shards, collective_id)
        return attend(tables, prefix_length, queries, keys, values, cache_pairs)

    attended, written = lax.cond(
        tables[MOST] <= FEW_PAGES,
        lambda: attention(FEW_PAGES, 2),
        lambda: attention(own_pages, 3),
    )
    layer_out, next_proj = chain(
        attended,
        residual_in,
        post_gain[None, :],
        next_gain[None, :],
        out_weight,
        gate_weight,
        up_weight,
        down_weight,
        next_weight,
        groups,
    )
    return (attended, written, layer_out, next_proj)


def solution(mesh):
    in_specs = (
        P(("tok", "grp"), None),
        P("tok", "grp"),
        P("tok", None),
        P("tok", None),
        P(),
        P(),
        P(),
        P("grp", None),
        P(),
        P(None, "grp"),
        P(None, "grp"),
        P("grp", None),
        P(),
        P(None, "grp"),
    )
    out_specs = (P("tok", "grp"), P("tok", "grp"), P(("tok", "grp"), None), P("tok", "grp"))
    return jax.shard_map(local, mesh=mesh, in_specs=in_specs, out_specs=out_specs, check_vma=False)
```

```python
import functools
import math

import jax
import jax.numpy as jnp
from jax import lax
from jax.experimental import pallas as pl
from jax.experimental.pallas import tpu as pltpu
from jax.sharding import PartitionSpec as P

HD = 256
PAGE = 16
TILE = 256
HALF = TILE // 2
MOST_PREFIX = 256
MESH = pl.DeviceIdType.MESH
VMEM_LIMIT = 60 * 1024 * 1024
FEW_PAGES = 7

masked_score = -1e30
lowest_peak = -1e20
norm_epsilon = 1e-05

START, LENGTH, SLOT, WHERE, SLOTS, COUNTS, MOST, TABLES = 0, 16, 32, 64, 320, 384, 448, 512

smem = pl.BlockSpec(memory_space=pltpu.SMEM)
vmem = pl.BlockSpec(memory_space=pltpu.VMEM)
hbm = pl.BlockSpec(memory_space=pl.ANY)


def shifted(value, size):
    return lax.shift_right_arithmetic(value, jnp.int32(size.bit_length() - 1))


def pack_kernel(
    shards,
    ids_ref,
    order_block_ref,
    prefix_ref,
    order_ref,
    fresh_ref,
    cache_ref,
    tiles,
    others,
    tables,
    tile_sem,
    page_sem,
):
    shard, group = lax.axis_index("tok"), lax.axis_index("grp")
    own_pages = order_ref.shape[0] // shards
    seg_count = prefix_ref.shape[0]
    side = group % 2
    pairs_at = (group // 2) * 2 * HD

    def columns(part):
        return pl.ds(pl.multiple_of(pairs_at + part * HD, HD), HD)

    def half_rows(which):
        return pl.ds(pl.multiple_of(which * HALF, HALF), HALF)

    fresh_copies = [
        pltpu.make_async_copy(
            fresh_ref.at[half_rows(side), columns(part)],
            tiles.at[part, pl.ds(0, HALF), :],
            tile_sem.at[part],
        )
        for part in range(2)
    ]
    fresh_copies.append(
        pltpu.make_async_copy(fresh_ref.at[half_rows(1 - side), columns(side)], others, tile_sem.at[2])
    )
    for copy in fresh_copies:
        copy.start()

    def page_copy(page, rank, part):
        return pltpu.make_async_copy(
            cache_ref.at[pl.ds(pl.multiple_of(page * PAGE, PAGE), PAGE), columns(part)],
            tiles.at[part, pl.ds(pl.multiple_of(HALF + rank * PAGE, PAGE), PAGE), :],
            page_sem.at[rank, part],
        )

    ids = ids_ref[...]
    starts = [jnp.int32(0)]
    for s in range(1, seg_count):
        starts.append(jnp.sum((ids < s).astype(jnp.float32)).astype(jnp.int32))
    starts.append(jnp.int32(ids_ref.shape[0] * ids_ref.shape[1]))
    slot = jnp.int32(0)
    for s in range(seg_count):
        length = starts[s + 1] - starts[s]
        tables[START + s] = starts[s]
        tables[LENGTH + s] = length
        tables[SLOT + s] = slot
        slot = slot + shifted(prefix_ref[s] + length + PAGE - 1, PAGE)
    tables[SLOT + seg_count] = slot

    for owner in range(2 * shards):
        tables[COUNTS + owner] = 0

    @pl.loop(0, seg_count)
    def _(s):
        first = tables[SLOT + s]

        @pl.loop(0, shifted(prefix_ref[s] + PAGE - 1, PAGE))
        def _(j):
            page = order_ref[first + j]
            owner = shifted(page, own_pages)
            parity = j & 1
            count = COUNTS + 2 * owner + parity
            rank = tables[count]
            tables[count] = rank + 1
            tables[WHERE + s * PAGE + j] = owner * own_pages + rank

            @pl.when((owner == shard) & (parity == side))
            def _():
                for part in range(2):
                    page_copy(page & (own_pages - 1), rank, part).start()

    most = jnp.int32(0)
    for owner in range(2 * shards):
        most = jnp.maximum(most, tables[COUNTS + owner])
    tables[MOST] = most

    order = order_block_ref[...]
    at = lax.broadcasted_iota(jnp.int32, order.shape, 0) * order.shape[1] + (
        lax.broadcasted_iota(jnp.int32, order.shape, 1)
    )
    at = at.astype(jnp.float32)
    for i in range(own_pages):
        mine = order == shard * own_pages + i
        tables[SLOTS + i] = jnp.sum(jnp.where(mine, at, 0.0)).astype(jnp.int32)

    @pl.loop(0, tables[COUNTS + 2 * shard + side])
    def _(rank):
        for part in range(2):
            page_copy(0, rank, part).wait()

    for copy in fresh_copies:
        copy.wait()


def pack(segment_ids, prefix_length, page_order, fresh, cache, shards):
    own_pages = page_order.shape[0] // shards
    return pl.pallas_call(
        functools.partial(pack_kernel, shards),
        out_shape=(
            jax.ShapeDtypeStruct((2, HALF + own_pages * PAGE, HD), jnp.bfloat16),
            jax.ShapeDtypeStruct((HALF, HD), jnp.bfloat16),
            jax.ShapeDtypeStruct((TABLES,), jnp.int32),
        ),
        in_specs=[vmem, vmem, smem, smem, hbm, hbm],
        out_specs=(vmem, vmem, smem),
        scratch_shapes=[
            pltpu.SemaphoreType.DMA((3,)),
            pltpu.SemaphoreType.DMA((own_pages, 2)),
        ],
        name="pack",
    )(
        segment_ids.reshape(-1, 128),
        page_order.reshape(-1, 128),
        prefix_length,
        page_order,
        fresh,
        cache,
    )


SIDE = 4
ROUTES = {
    (0, 0): ("p+", "p-", "q+", "q-", "core"),
    (3, 0): ("q+", "q-", "p+", "core"),
    (1, 0): ("q+", "q-", "core"),
    (0, 3): ("q+", "core"),
    (0, 1): ("core",),
    (2, 0): ("q+", "q-", "core"),
    (3, 3): ("q+", "core"),
    (3, 1): ("core",),
    (1, 3): ("core",),
    (1, 1): ("q-", "core"),
    (0, 2): ("core",),
    (2, 3): ("core",),
    (2, 1): ("q-", "core"),
    (3, 2): ("core",),
    (1, 2): ("core",),
    (2, 2): ("core",),
}
MOVES = {"p+": (1, 0), "p-": (-1, 0), "q+": (0, 1), "q-": (0, -1), "core": (0, 0)}
TILES = list(ROUTES)
MESSAGES = [(tile, way) for tile, ways in ROUTES.items() for way in ways]
Z_LAG = 3


def arrival(tile):
    for index, (sent, way) in enumerate(MESSAGES):
        move = MOVES[way]
        if way != "core" and ((sent[0] - move[0]) % SIDE, (sent[1] - move[1]) % SIDE) == tile:
            return index
    return None


def spread_kernel(
    rows,
    tiles_ref,
    others_ref,
    query_ref,
    pairs,
    rest,
    other_query,
    own,
    own_rest,
    send_sem,
    recv_sem,
    z_send,
    z_recv,
    core_send,
    core_recv,
    own_sem,
):
    shard, group = lax.axis_index("tok"), lax.axis_index("grp")
    side = group % 2
    partner = group + 1 - 2 * side
    core, x, y = shard % 2, (shard // 2) % SIDE, shard // (2 * SIDE)

    def shard_at(dx, dy, c):
        return (((y + dy + SIDE) % SIDE) * SIDE + (x + dx + SIDE) % SIDE) * 2 + c

    def place(part, p, q, c):
        return shard_at(p, q, c) if part == 0 else shard_at(q, p, c)

    def remote(source, target, send, recv, device):
        return pltpu.make_async_remote_copy(
            src_ref=source,
            dst_ref=target,
            send_sem=send,
            recv_sem=recv,
            device_id=device,
            device_id_type=MESH,
        )

    def message(part, index):
        tile, way = MESSAGES[index]
        move = MOVES[way]
        target = place(part, move[0], move[1], 1 - core if way == "core" else core)
        block = pairs.at[part, place(part, tile[0], tile[1], core)]
        source = tiles_ref.at[part, pl.ds(0, rows), :] if tile == (0, 0) else block
        sems = send_sem.at[part, index], recv_sem.at[part, index]
        return remote(source, block, *sems, {"tok": target})

    def z_message(n):
        p, q = TILES[n]
        there = shard_at(p * side + q * (1 - side), q * side + p * (1 - side), core)
        source = pairs.at[1 - side, there, pl.ds(0, HALF), :]
        return remote(source, rest.at[there], z_send.at[n], z_recv.at[n], {"grp": partner})

    def landing(n):
        p, q = TILES[n]
        return rest.at[shard_at(p * (1 - side) + q * side, q * (1 - side) + p * side, core)]

    def core_message(n):
        block = rest.at[shard] if n == 0 else landing(n)
        source = others_ref if n == 0 else block
        device = {"tok": shard_at(0, 0, 1 - core)}
        return remote(source, block, core_send.at[n], core_recv.at[n], device)

    query_message = remote(query_ref, other_query, z_send.at[0], z_recv.at[0], {"grp": partner})
    fetches = [
        pltpu.make_async_copy(tiles_ref.at[part, pl.ds(0, rows), :], own.at[part], own_sem.at[part])
        for part in range(2)
    ] + [pltpu.make_async_copy(others_ref, own_rest, own_sem.at[2])]
    stores = [
        pltpu.make_async_copy(own.at[part], pairs.at[part, shard], own_sem.at[part])
        for part in range(2)
    ] + [pltpu.make_async_copy(own_rest, rest.at[shard], own_sem.at[2])]

    barrier = pltpu.get_barrier_semaphore()
    peers = [shard_at(1, 0, core), shard_at(-1, 0, core), shard_at(0, 1, core)]
    peers += [shard_at(0, -1, core), shard_at(0, 0, 1 - core)]
    devices = [{"tok": peer} for peer in peers] + [{"grp": partner}]
    for device in devices:
        pl.semaphore_signal(barrier, inc=1, device_id=device, device_id_type=MESH)
    for fetch in fetches:
        fetch.start()
    pl.semaphore_wait(barrier, len(devices))

    def pass_rest(n):
        block = landing(n)
        remote(block, block, z_send.at[n], z_recv.at[n], {"grp": partner}).wait_recv()
        core_message(n).start()

    for n, tile in enumerate(TILES):
        sent = [i for i, (t, _) in enumerate(MESSAGES) if t == tile]
        for part in range(2):
            if n > 0:
                message(part, arrival(tile)).wait_recv()
            for i in sent:
                message(part, i).start()
        if n == 0:
            query_message.start()
            core_message(0).start()
        else:
            z_message(n).start()
        if n > Z_LAG:
            pass_rest(n - Z_LAG)
    for n in range(len(TILES) - Z_LAG, len(TILES)):
        pass_rest(n)
    for fetch, store in zip(fetches, stores):
        fetch.wait()
        store.start()
    for store in stores:
        store.wait()
    query_message.wait()
    for part in range(2):
        for i, (_, way) in enumerate(MESSAGES):
            if way == "core":
                message(part, i).wait_recv()
    for n in range(len(TILES)):
        core_message(n).wait_recv()
        core_message(n).wait_send()
        if n > 0:
            z_message(n).wait_send()
    for part in range(2):
        for i in range(len(MESSAGES)):
            message(part, i).wait_send()


def spread(tiles, others, queries, rows, shards, collective_id):
    many = pltpu.SemaphoreType.DMA((2, len(MESSAGES)))
    few = pltpu.SemaphoreType.DMA((len(TILES),))
    return pl.pallas_call(
        functools.partial(spread_kernel, rows),
        out_shape=(
            jax.ShapeDtypeStruct((2, shards, rows, HD), jnp.bfloat16),
            jax.ShapeDtypeStruct((shards, HALF, HD), jnp.bfloat16),
            jax.ShapeDtypeStruct(queries.shape, jnp.bfloat16),
        ),
        in_specs=[hbm] * 3,
        out_specs=(hbm, hbm, hbm),
        scratch_shapes=[
            pltpu.VMEM((2, rows, HD), jnp.bfloat16),
            pltpu.VMEM((HALF, HD), jnp.bfloat16),
            many,
            many,
            few,
            few,
            few,
            few,
            pltpu.SemaphoreType.DMA((3,)),
        ],
        compiler_params=pltpu.CompilerParams(collective_id=collective_id, has_side_effects=True),
        name="spread",
    )(tiles, others, queries)


STEP_TILES = 4
PAGE_STEP = 4


def attend_kernel(
    seg_count,
    tables,
    prefix_ref,
    q_ref,
    other_q_ref,
    pairs_ref,
    rest_ref,
    cache_ref,
    own_ref,
    other_ref,
    own_stats,
    other_stats,
    written_ref,
    tiles,
    prefix_tile,
    windows,
    query,
    peak,
    total,
    acc,
    place_seg,
    tile_sem,
    page_sem,
    window_sem,
    cache_sem,
):
    shard, group = lax.axis_index("tok"), lax.axis_index("grp")
    side = group % 2
    rows = q_ref.shape[0]
    own_pages = written_ref.shape[0] // PAGE
    shards = pairs_ref.shape[1]
    wide = STEP_TILES * HALF
    blocks = TILE // PAGE

    def cache_copy():
        columns = pl.ds(pl.multiple_of(group * HD, HD), HD)
        return pltpu.make_async_copy(cache_ref.at[:, columns], written_ref, cache_sem)

    def page_place(i, seg):
        position = (tables[SLOTS + i] - tables[SLOT + seg]) * PAGE
        return position, tables[START + seg] + position - prefix_ref[seg]

    def window_copy(source, i, which):
        return pltpu.make_async_copy(
            source, windows.at[i, pl.ds(which * PAGE, PAGE), :], window_sem.at[i, which]
        )

    def tile_copy(index, slot, n, part):
        return pltpu.make_async_copy(
            pairs_ref.at[part, jnp.maximum(index, 0), pl.ds(0, HALF), :],
            tiles.at[slot, part, pl.ds(n * HALF, HALF), :],
            tile_sem.at[slot, n, part],
        )

    def page_copy(seg, i, part):
        place = tables[WHERE + seg * PAGE + 2 * i + side]
        row = HALF + (place & (own_pages - 1)) * PAGE
        return pltpu.make_async_copy(
            pairs_ref.at[part, shifted(place, own_pages), pl.ds(pl.multiple_of(row, PAGE), PAGE), :],
            prefix_tile.at[part, pl.ds(pl.multiple_of(i * PAGE, PAGE), PAGE), :],
            page_sem.at[i, part],
        )

    first_row = shard * rows
    seg_lo = jnp.int32(-1)
    seg_hi = jnp.int32(-1)
    for s in range(seg_count):
        seg_lo = seg_lo + (tables[START + s] <= first_row).astype(jnp.int32)
        seg_hi = seg_hi + (tables[START + s] <= first_row + rows - 1).astype(jnp.int32)
    first_tile = shifted(tables[START + seg_lo], TILE)
    last_low = tables[START + seg_hi]
    steps = shifted(shard - first_tile, STEP_TILES) + 1
    base = shard + 1 - STEP_TILES * steps

    def start_tiles(step):
        for n in range(STEP_TILES):
            for part in range(2):
                tile_copy(base + STEP_TILES * step + n, step & 1, n, part).start()

    start_tiles(0)
    cache_copy().start()

    @pl.loop(0, own_pages)
    def _(i):
        slot = tables[SLOTS + i]
        seg = jnp.int32(-1)
        for s in range(seg_count):
            seg = seg + (tables[SLOT + s] <= slot).astype(jnp.int32)
        place_seg[i] = seg
        _, token = page_place(i, seg)
        first = shifted(token, PAGE)
        for which in range(2):
            block = jnp.clip(first + which, 0, shards * blocks - 1)
            tile, within = shifted(block, blocks), block & (blocks - 1)
            here = shifted(within, blocks // 2) == side
            row = pl.ds(pl.multiple_of((within & (blocks // 2 - 1)) * PAGE, PAGE), PAGE)

            @pl.when(here)
            def _():
                window_copy(pairs_ref.at[side, tile, row, :], i, which).start()

            @pl.when(jnp.logical_not(here))
            def _():
                window_copy(rest_ref.at[tile, row, :], i, which).start()

    prefix_tile[...] = jnp.zeros_like(prefix_tile)
    peak[...] = jnp.full_like(peak, lowest_peak)
    total[...] = jnp.zeros_like(total)
    acc[...] = jnp.zeros_like(acc)
    for n, source in enumerate((q_ref, other_q_ref)):
        query[pl.ds(n * rows, rows), :] = (
            source[...].astype(jnp.float32) * (1.0 / math.sqrt(HD))
        ).astype(jnp.bfloat16)
    row_at = first_row + (lax.broadcasted_iota(jnp.int32, (2 * rows, 1), 0) & (rows - 1))
    low = jnp.zeros((2 * rows, 1), jnp.int32)
    seg_at = jnp.full((2 * rows, 1), -1, jnp.int32)
    for s in range(seg_count):
        begun = row_at >= tables[START + s]
        low = jnp.where(begun, tables[START + s], low)
        seg_at = seg_at + begun.astype(jnp.int32)

    def absorb(keys, values, live):
        scores = lax.dot_general(
            query[...], keys, (((1,), (1,)), ((), ())), preferred_element_type=jnp.float32
        )
        if live is not None:
            scores = jnp.where(live, scores, masked_score)
        before = peak[...]
        raised = jnp.maximum(before, jnp.max(scores, axis=1, keepdims=True))
        weights = jnp.exp(scores - raised)
        rescale = jnp.exp(before - raised)
        peak[...] = raised
        total[...] = total[...] * rescale + jnp.sum(weights, axis=1, keepdims=True)
        acc[...] = acc[...] * rescale + jnp.dot(
            weights.astype(jnp.bfloat16), values, preferred_element_type=jnp.float32
        )

    @pl.loop(0, steps)
    def _(step):
        slot = step & 1
        for n in range(STEP_TILES):
            for part in range(2):
                tile_copy(base + STEP_TILES * step + n, slot, n, part).wait()

        @pl.when(step + 1 < steps)
        def _():
            start_tiles(step + 1)

        at = (base + STEP_TILES * step) * TILE
        whole = (at >= last_low) & (step + 1 < steps)

        @pl.when(whole)
        def _():
            absorb(tiles[slot, 0], tiles[slot, 1], None)

        @pl.when(jnp.logical_not(whole))
        def _():
            column = lax.broadcasted_iota(jnp.int32, (1, wide), 1)
            key_at = at + shifted(column, HALF) * TILE + side * HALF + (column & (HALF - 1))
            absorb(tiles[slot, 0], tiles[slot, 1], (key_at >= low) & (key_at <= row_at))

    @pl.loop(seg_lo, seg_hi + 1)
    def _(seg):
        pages = shifted(prefix_ref[seg] + PAGE - 1, PAGE)
        count = shifted(pages + 1 - side, 2)

        @pl.loop(0, count)
        def _(i):
            for part in range(2):
                page_copy(seg, i, part).start()

        @pl.loop(0, count)
        def _(i):
            for part in range(2):
                page_copy(seg, i, part).wait()

        @pl.when(count > 0)
        def _():
            column = lax.broadcasted_iota(jnp.int32, (1, prefix_tile.shape[1]), 1)
            at = (2 * shifted(column, PAGE) + side) * PAGE + (column & (PAGE - 1))
            absorb(prefix_tile[0], prefix_tile[1], (seg_at == seg) & (at < prefix_ref[seg]))

    summed = total[...]
    part = acc[...] / jnp.where(summed > 0.0, summed, 1.0)
    own_ref[...] = part[:rows]
    other_ref[...] = part[rows:].astype(jnp.bfloat16)
    line = lax.broadcasted_iota(jnp.int32, (128, 128), 0)
    diagonal = line == lax.broadcasted_iota(jnp.int32, (128, 128), 1)
    for n, stats in enumerate((own_stats, other_stats)):
        stats[...] = jnp.zeros_like(stats)
        for m, column in enumerate((peak, total)):
            for r in range(rows // 128):
                values = column[pl.ds(n * rows + r * 128, 128), :]
                spread_out = jnp.where(diagonal, values, 0.0)
                stats[pl.ds(m * (rows // 128) + r, 1), :] = jnp.sum(
                    spread_out, axis=0, keepdims=True
                )

    cache_copy().wait()

    @pl.loop(0, own_pages // PAGE_STEP)
    def _(group_of_pages):
        for n in range(PAGE_STEP):
            i = group_of_pages * PAGE_STEP + n
            seg = place_seg[i]
            position, token = page_place(i, seg)
            for which in range(2):
                window_copy(rest_ref.at[0, pl.ds(0, PAGE), :], i, which).wait()
            shift = token & (PAGE - 1)
            to = lax.broadcasted_iota(jnp.int32, (PAGE, 2 * PAGE), 0)
            taken = lax.broadcasted_iota(jnp.int32, (PAGE, 2 * PAGE), 1)
            picked = (taken == to + shift).astype(jnp.bfloat16)
            fresh = jnp.dot(picked, windows[i], preferred_element_type=jnp.float32)
            at = position + lax.broadcasted_iota(jnp.int32, (PAGE, HD), 0)
            used = tables[SLOTS + i] < tables[SLOT + seg_count]
            until = jnp.where(used, prefix_ref[seg] + tables[LENGTH + seg], 0)
            live = (at >= prefix_ref[seg]) & (at < until)
            block = pl.ds(pl.multiple_of(i * PAGE, PAGE), PAGE)
            held = written_ref[block, :].astype(jnp.float32)
            written_ref[block, :] = jnp.where(live, fresh, held).astype(jnp.bfloat16)


def attend(tables, prefix_length, queries, other_queries, pairs, rest, cache):
    rows = queries.shape[0]
    most = MOST_PREFIX // 2
    own_pages = cache.shape[0] // PAGE
    stats = jax.ShapeDtypeStruct((8, 128), jnp.float32)
    return pl.pallas_call(
        functools.partial(attend_kernel, prefix_length.shape[0]),
        out_shape=(
            jax.ShapeDtypeStruct((rows, HD), jnp.float32),
            jax.ShapeDtypeStruct((rows, HD), jnp.bfloat16),
            stats,
            stats,
            jax.ShapeDtypeStruct((cache.shape[0], HD), jnp.bfloat16),
        ),
        in_specs=[smem, smem, vmem, vmem, hbm, hbm, hbm],
        out_specs=(vmem,) * 5,
        scratch_shapes=[
            pltpu.VMEM((2, 2, STEP_TILES * HALF, HD), jnp.bfloat16),
            pltpu.VMEM((2, most, HD), jnp.bfloat16),
            pltpu.VMEM((own_pages, 2 * PAGE, HD), jnp.bfloat16),
            pltpu.VMEM((2 * rows, HD), jnp.bfloat16),
            pltpu.VMEM((2 * rows, 1), jnp.float32),
            pltpu.VMEM((2 * rows, 1), jnp.float32),
            pltpu.VMEM((2 * rows, HD), jnp.float32),
            pltpu.SMEM((own_pages,), jnp.int32),
            pltpu.SemaphoreType.DMA((2, STEP_TILES, 2)),
            pltpu.SemaphoreType.DMA((most // PAGE, 2)),
            pltpu.SemaphoreType.DMA((own_pages, 2)),
            pltpu.SemaphoreType.DMA(()),
        ],
        name="attend",
    )(tables, prefix_length, queries, other_queries, pairs, rest, cache)


def chain_kernel(
    groups,
    own_ref,
    other_ref,
    own_stats,
    other_stats,
    residual_ref,
    post_gain_ref,
    next_gain_ref,
    wo_hbm,
    wg_hbm,
    wu_hbm,
    wd_hbm,
    wn_hbm,
    attended_ref,
    layer_ref,
    next_ref,
    part_in,
    stats_in,
    wo,
    wg,
    wu,
    wd,
    wn,
    partial,
    hidden,
    sums,
    outgoing,
    incoming,
    gathered,
    weight_sem,
    part_send,
    part_recv,
    sum_send,
    sum_recv,
    copy_send,
    copy_recv,
):
    me = lax.axis_index("grp")
    width = layer_ref.shape[1]
    chunk = layer_ref.shape[0]
    half = width // 2
    far = groups // 2
    steps = (1, -1)
    neighbour = [lax.rem(me + 1, groups), lax.rem(me + groups - 1, groups)]

    loads = []
    for i, (source, target) in enumerate(
        ((wo_hbm, wo), (wg_hbm, wg), (wu_hbm, wu), (wd_hbm, wd), (wn_hbm, wn))
    ):
        loads.append(pltpu.make_async_copy(source, target, weight_sem.at[i]))
        loads[i].start()

    barrier = pltpu.get_barrier_semaphore()
    for d in range(2):
        pl.semaphore_signal(
            barrier, inc=1, device_id={"grp": neighbour[d]}, device_id_type=MESH
        )
    pl.semaphore_wait(barrier, 2)

    swaps = [
        pltpu.make_async_remote_copy(
            src_ref=source,
            dst_ref=target,
            send_sem=part_send.at[i],
            recv_sem=part_recv.at[i],
            device_id={"grp": me + 1 - 2 * (me % 2)},
            device_id_type=MESH,
        )
        for i, (source, target) in enumerate(((other_stats, stats_in), (other_ref, part_in)))
    ]
    for swap in swaps:
        swap.start()

    def rows_of(owner):
        index = lax.rem(owner + 2 * groups, groups)
        return pl.ds(pl.multiple_of(index * chunk, chunk), chunk)

    def columns_of(h):
        return pl.ds(h * half, half)

    def sum_copy(phase, d, h, s):
        return pltpu.make_async_remote_copy(
            src_ref=outgoing.at[phase, d, h, s],
            dst_ref=incoming.at[phase, d, h, s],
            send_sem=sum_send.at[phase, d, h, s],
            recv_sem=sum_recv.at[phase, d, h, s],
            device_id={"grp": neighbour[d]},
            device_id_type=MESH,
        )

    def gather_copy(phase, d, h, k):
        block = gathered.at[phase, rows_of(me - steps[d] * k), columns_of(h)]
        return pltpu.make_async_remote_copy(
            src_ref=block,
            dst_ref=block,
            send_sem=copy_send.at[phase, d, h, k],
            recv_sem=copy_recv.at[phase, d, h, k],
            device_id={"grp": neighbour[d]},
            device_id_type=MESH,
        )

    def reduce_scatter(phase):
        for s in range(far):
            for h in range(2):
                for d in range(2):
                    first = 0 if h == d else 1
                    if s < first:
                        continue
                    owner = me + steps[d] * (far - s)
                    value = partial[rows_of(owner), columns_of(h)]
                    if s > first:
                        sum_copy(phase, d, h, s - 1).wait_recv()
                        value = value + incoming[phase, d, h, s - 1].astype(jnp.float32)
                    outgoing[phase, d, h, s] = value.astype(jnp.bfloat16)
                    sum_copy(phase, d, h, s).start()
        for h in range(2):
            value = partial[rows_of(me), columns_of(h)]
            for d in range(2):
                sum_copy(phase, d, h, far - 1).wait_recv()
                value = value + incoming[phase, d, h, far - 1].astype(jnp.float32)
            sums[:, columns_of(h)] = value
        for s in range(far):
            for h in range(2):
                for d in range(2):
                    if s >= (0 if h == d else 1):
                        sum_copy(phase, d, h, s).wait_send()

    def all_gather(phase):
        for k in range(far):
            for h in range(2):
                for d in range(2):
                    if k >= (far if h == d else far - 1):
                        continue
                    if k > 0:
                        gather_copy(phase, d, h, k - 1).wait_recv()
                    gather_copy(phase, d, h, k).start()
        for h in range(2):
            for d in range(2):
                gather_copy(phase, d, h, (far if h == d else far - 1) - 1).wait_recv()
        for k in range(far):
            for h in range(2):
                for d in range(2):
                    if k < (far if h == d else far - 1):
                        gather_copy(phase, d, h, k).wait_send()

    def normed(values, gain_ref):
        scaled = values * lax.rsqrt(
            jnp.mean(values * values, axis=-1, keepdims=True) + norm_epsilon
        )
        return (scaled * gain_ref[...]).astype(jnp.bfloat16)

    rows = attended_ref.shape[0]
    line = lax.broadcasted_iota(jnp.int32, (128, 128), 0)
    diagonal = line == lax.broadcasted_iota(jnp.int32, (128, 128), 1)

    def column_of(stats, row):
        values = jnp.broadcast_to(stats[pl.ds(row, 1), :], (128, 128))
        return jnp.sum(jnp.where(diagonal, values, 0.0), axis=1, keepdims=True)

    for swap in swaps:
        swap.wait_recv()
    blocks = rows // 128
    for r in range(blocks):
        peaks = [column_of(stats, r) for stats in (own_stats, stats_in)]
        totals = [column_of(stats, blocks + r) for stats in (own_stats, stats_in)]
        highest = jnp.maximum(peaks[0], peaks[1])
        shares = [t * jnp.exp(p - highest) for p, t in zip(peaks, totals)]
        block = pl.ds(r * 128, 128)
        merged = own_ref[block, :] * shares[0] + part_in[block, :].astype(jnp.float32) * shares[1]
        attended_ref[block, :] = (merged / (shares[0] + shares[1])).astype(jnp.bfloat16)
    for swap in swaps:
        swap.wait_send()

    loads[0].wait()

    @pl.loop(0, width // 256)
    def _(j):
        columns = pl.ds(pl.multiple_of(j * 256, 256), 256)
        partial[:, columns] = jnp.dot(
            attended_ref[...], wo[:, columns], preferred_element_type=jnp.float32
        )

    reduce_scatter(0)
    first_sum = (residual_ref[...].astype(jnp.float32) + sums[...]).astype(jnp.bfloat16)
    layer_ref[...] = first_sum
    gathered[0, rows_of(me), :] = normed(first_sum.astype(jnp.float32), post_gain_ref)
    all_gather(0)

    loads[1].wait()
    loads[2].wait()

    @pl.loop(0, wg.shape[1] // 256)
    def _(j):
        columns = pl.ds(pl.multiple_of(j * 256, 256), 256)
        rows = gathered[0]
        gate = jnp.dot(rows, wg[:, columns], preferred_element_type=jnp.float32)
        up = jnp.dot(rows, wu[:, columns], preferred_element_type=jnp.float32)
        hidden[:, columns] = (jax.nn.silu(gate) * up).astype(jnp.bfloat16)

    loads[3].wait()

    @pl.loop(0, width // 256)
    def _(j):
        columns = pl.ds(pl.multiple_of(j * 256, 256), 256)
        partial[:, columns] = jnp.dot(
            hidden[...], wd[:, columns], preferred_element_type=jnp.float32
        )

    reduce_scatter(1)
    layer_out = (layer_ref[...].astype(jnp.float32) + sums[...]).astype(jnp.bfloat16)
    layer_ref[...] = layer_out
    gathered[1, rows_of(me), :] = normed(layer_out.astype(jnp.float32), next_gain_ref)
    all_gather(1)

    loads[4].wait()

    @pl.loop(0, wn.shape[1] // 256)
    def _(j):
        columns = pl.ds(pl.multiple_of(j * 256, 256), 256)
        next_ref[:, columns] = jnp.dot(
            gathered[1], wn[:, columns], preferred_element_type=jnp.float32
        ).astype(jnp.bfloat16)


def chain(parts, residual, post_gain, next_gain, wo, wg, wu, wd, wn, groups):
    rows = parts[0].shape[0]
    chunk, width = residual.shape
    far = groups // 2
    messages = (2, 2, 2, far)
    return pl.pallas_call(
        functools.partial(chain_kernel, groups),
        out_shape=(
            jax.ShapeDtypeStruct((rows, HD), jnp.bfloat16),
            jax.ShapeDtypeStruct((chunk, width), jnp.bfloat16),
            jax.ShapeDtypeStruct((rows, wn.shape[1]), jnp.bfloat16),
        ),
        in_specs=[vmem] * 7 + [hbm] * 5,
        out_specs=(vmem, vmem, vmem),
        scratch_shapes=[
            pltpu.VMEM((rows, HD), jnp.bfloat16),
            pltpu.VMEM((8, 128), jnp.float32),
        ]
        + [pltpu.VMEM(w.shape, w.dtype) for w in (wo, wg, wu, wd, wn)]
        + [
            pltpu.VMEM((rows, width), jnp.float32),
            pltpu.VMEM((rows, wg.shape[1]), jnp.bfloat16),
            pltpu.VMEM((chunk, width), jnp.float32),
            pltpu.VMEM(messages + (chunk, width // 2), jnp.bfloat16),
            pltpu.VMEM(messages + (chunk, width // 2), jnp.bfloat16),
            pltpu.VMEM((2, rows, width), jnp.bfloat16),
            pltpu.SemaphoreType.DMA((5,)),
            pltpu.SemaphoreType.DMA((2,)),
            pltpu.SemaphoreType.DMA((2,)),
            pltpu.SemaphoreType.DMA(messages),
            pltpu.SemaphoreType.DMA(messages),
            pltpu.SemaphoreType.DMA(messages),
            pltpu.SemaphoreType.DMA(messages),
        ],
        compiler_params=pltpu.CompilerParams(
            collective_id=1, has_side_effects=True, vmem_limit_bytes=VMEM_LIMIT
        ),
        name="chain",
    )(*parts, residual, post_gain, next_gain, wo, wg, wu, wd, wn)


def copy_kernel(*refs):
    count = len(refs) // 2
    for source, target in zip(refs[:count], refs[count:]):
        target[...] = source[...]


def local(
    residual_in,
    queries,
    fresh_pairs,
    cache_pairs,
    segment_ids,
    prefix_length,
    page_order,
    out_weight,
    post_gain,
    gate_weight,
    up_weight,
    down_weight,
    next_gain,
    next_weight,
):
    groups, shards = lax.axis_size("grp"), lax.axis_size("tok")
    own_pages = page_order.shape[0] // shards
    tiles, others, tables = pack(
        segment_ids, prefix_length, page_order, fresh_pairs, cache_pairs, shards
    )

    def attention(pages, collective_id):
        rows = HALF + pages * PAGE
        pairs, rest, other_queries = spread(tiles, others, queries, rows, shards, collective_id)
        return attend(tables, prefix_length, queries, other_queries, pairs, rest, cache_pairs)

    *parts, written = lax.cond(
        tables[MOST] <= FEW_PAGES,
        lambda: attention(FEW_PAGES, 2),
        lambda: attention(own_pages, 3),
    )
    results = chain(
        (parts[0], parts[1], parts[2], parts[3]),
        residual_in,
        post_gain[None, :],
        next_gain[None, :],
        out_weight,
        gate_weight,
        up_weight,
        down_weight,
        next_weight,
        groups,
    )
    attended, layer_out, next_proj = pl.pallas_call(
        copy_kernel,
        out_shape=tuple(jax.ShapeDtypeStruct(a.shape, a.dtype) for a in results),
        in_specs=[vmem] * 3,
        out_specs=(vmem,) * 3,
        name="results",
    )(*results)
    return (attended, written, layer_out, next_proj)


def solution(mesh):
    in_specs = (
        P(("tok", "grp"), None),
        P("tok", "grp"),
        P("tok", None),
        P("tok", None),
        P(),
        P(),
        P(),
        P("grp", None),
        P(),
        P(None, "grp"),
        P(None, "grp"),
        P("grp", None),
        P(),
        P(None, "grp"),
    )
    out_specs = (P("tok", "grp"), P("tok", "grp"), P(("tok", "grp"), None), P("tok", "grp"))
    return jax.shard_map(local, mesh=mesh, in_specs=in_specs, out_specs=out_specs, check_vma=False)
```
